256 devices in a mesh: dp: 8 (over x, y_hi), row: 32 (over y_lo, z, core).
Axes of the slice: x: 4, y: 4 (y_hi: 2, y_lo: 2; y = y_hi * 2 + y_lo), z: 8, core: 2. Of those that a mesh axis runs over, the one named last changes fastest.
Arguments:
- patch_queries: bfloat16 [8, 4096, 512], P('dp', 'row'), may hold values from -6 to 6
- patch_keys: bfloat16 [8, 4096, 512], P('dp', 'row'), may hold values from -6 to 6
- scan_input: float32 [8, 4096, 512], P('dp', 'row'), may hold values from -6 to 6
- decay_rate: float32 [8, 4096, 512], P('dp', 'row'), may hold values from 0.4 to 1, as said below
- gate_logit: bfloat16 [8, 4096, 512], P('dp', 'row'), may hold values from -6 to 6
- grad_output: bfloat16 [8, 4096, 1024], P('dp', 'row'), may hold values from -6 to 6
- output_weight: bfloat16 [1024, 512], replicated, may hold values from -0.25 to 0.25
Outputs:
- grad_queries: bfloat16 [8, 4096, 512], P('dp', 'row')
- grad_keys: bfloat16 [8, 4096, 512], P('dp', 'row')
- grad_input: float32 [8, 4096, 512], P('dp', 'row')
- grad_decay: float32 [8, 4096, 512], P('dp', 'row')
- grad_gate: bfloat16 [8, 4096, 512], P('dp', 'row')
- grad_weight: float32 [1024, 512], P(('dp', 'row'))
The draws below stay inside these ranges and needn't reach their ends.
Inputs may be any that keep to these rules, and one draw needn't show every extreme that they name: `decay_rate`: forget gates lie strictly below 1.
All inputs are finite; a program needn't handle non-finite values.
Results may differ from the reference program's by a relative error of at most 0.012.
The reference program's roundings to bfloat16 on the way (of `value_low`, `grad_attended`, `weights_low`, `attended`, `weighted` and `grad_scores`) count: a program that leaves them out, or rounds other values in their place, can miss the bound.
Values may be sent and summed in bfloat16 or wider, within the bound.
No kernel may reach another device: no remote copies, remote signals or barrier semaphores. Data moves between devices by JAX's collectives and lax.ppermute only.
A program may use at most 128 MiB of HBM per device.

```python
import math
import jax
import jax.numpy as jnp
from jax import lax

D = 1024
HEADS = 8
HEAD_DIM = 64
ROWS_DEV = 128
CH = 512
PATCH_TOKENS = 4096
IMAGE_TOTAL = 8


def draw_rows(image_key, salt):
    noise = jax.random.normal(jax.random.fold_in(image_key, salt), (PATCH_TOKENS, CH), jnp.float32)
    lower, upper = (0.4, 1.6)
    spread = jnp.exp(jax.random.uniform(jax.random.fold_in(image_key, salt + 1), (PATCH_TOKENS, 1), jnp.float32, math.log(lower), math.log(upper)))
    return jnp.clip(noise * spread, -6.0, 6.0)


def image_keys_of(key):
    return jax.vmap(lambda number: jax.random.fold_in(key, number))(jnp.arange(IMAGE_TOTAL))


def draw_patch_queries(key, part):

    def one_image(image_key):
        rows_drawn = draw_rows(image_key, 11)
        return rows_drawn
    return jax.vmap(one_image)(image_keys_of(key)).astype(jnp.bfloat16)


def draw_patch_keys(key, part):

    def one_image(image_key):
        rows_drawn = draw_rows(image_key, 21)
        return rows_drawn
    return jax.vmap(one_image)(image_keys_of(key)).astype(jnp.bfloat16)


def draw_decay_rate(key, part):
    slow_count = CH // 2
    order = jax.random.permutation(jax.random.fold_in(key, 31), CH)
    slow = order < slow_count
    slow_rate = jnp.exp(jax.random.uniform(jax.random.fold_in(key, 32), (CH,), jnp.float32, math.log(0.03), math.log(0.25))) / PATCH_TOKENS
    fast_rate = jnp.exp(jax.random.uniform(jax.random.fold_in(key, 33), (CH,), jnp.float32, math.log(1.0 / 50.0), math.log(1.0 / 30.0)))
    channel_rate = jnp.where(slow, slow_rate, fast_rate)
    token_factor = jnp.exp(jax.random.uniform(jax.random.fold_in(key, 34), (IMAGE_TOTAL, PATCH_TOKENS, CH), jnp.float32, -0.7, 0.7))
    block_factor = jnp.exp(jax.random.uniform(jax.random.fold_in(key, 35), (IMAGE_TOTAL, PATCH_TOKENS // ROWS_DEV, 1, CH), jnp.float32, -0.5, 0.5))
    block_factor = jnp.broadcast_to(block_factor, (IMAGE_TOTAL, PATCH_TOKENS // ROWS_DEV, ROWS_DEV, CH)).reshape(IMAGE_TOTAL, PATCH_TOKENS, CH)
    decay_factor = jnp.exp(-channel_rate * token_factor * block_factor)
    spike_position = jax.random.randint(jax.random.fold_in(key, 36), (IMAGE_TOTAL, 2, 1), 1, PATCH_TOKENS)
    spike_mask = jnp.any(jnp.arange(PATCH_TOKENS)[None, None, :] == spike_position, axis=1)
    retained_fraction = jax.random.uniform(jax.random.fold_in(key, 37), (IMAGE_TOTAL, PATCH_TOKENS, CH), jnp.float32, 0.5, 0.8)
    return decay_factor * jnp.where(spike_mask[:, :, None], retained_fraction, 1.0)


def with_spikes(values, rng, source, target, shards_of, factor):
    owner, partner = [(jnp.arange(values.shape[dim]) // (values.shape[dim] // shards_of)).reshape([-1 if axis == dim else 1 for axis in range(values.ndim)]) for dim in (source, target)]
    chosen = jax.random.permutation(rng, shards_of)[partner]
    strong = (owner == chosen) | (owner == (partner + shards_of // 2) % shards_of)
    return jnp.where(strong, factor * values, values)


def level_of(rng, shape, shards, least, top_value):
    factor_of, own = 1.0, jax.random.fold_in(rng, 6)
    for position, parts in shards:
        heights = jnp.exp(jax.random.uniform(jax.random.fold_in(own, position), (parts,), jnp.float32, least / len(shards), top_value / len(shards)))
        factor_of = factor_of * jnp.repeat(heights, shape[position] // parts).reshape([-1 if axis == position else 1 for axis in range(len(shape))])
    return factor_of


def bell_draw(stream_key, dims, scale, bound, pieces=(), held_as=jnp.bfloat16):
    values = scale * jax.random.normal(stream_key, dims, jnp.float32)
    if pieces:
        values = values * level_of(stream_key, dims, pieces, -0.22, 0.18)
    return jnp.clip(values, -bound, bound).astype(held_as)


def gaussian_with(rng, dims, deviation, bound, pieces, heavy, kind=jnp.bfloat16):
    values = deviation * jax.random.normal(rng, dims, jnp.float32)
    if pieces:
        values = values * level_of(rng, dims, pieces, -0.22, 0.18)
    return jnp.clip(with_spikes(values, jax.random.fold_in(rng, 3), *heavy), -bound, bound).astype(kind)


def setup_inputs(seed: int = 0) -> dict:
    keys = jax.random.split(jax.random.key(seed), 8)
    patch_queries = draw_patch_queries(jax.random.fold_in(keys[7], 71), 0)
    patch_keys = draw_patch_keys(jax.random.fold_in(keys[7], 71), 0)
    scan_input = bell_draw(keys[2], (IMAGE_TOTAL, PATCH_TOKENS, CH), 1.0, 6.0, ((0, 8), (1, 32)), jnp.float32)
    decay_rate = draw_decay_rate(jax.random.fold_in(keys[7], 71), 0)
    gate_logit = bell_draw(keys[4], (IMAGE_TOTAL, PATCH_TOKENS, CH), 1.0, 6.0, ((0, 8), (1, 32)))
    grad_output = gaussian_with(keys[5], (IMAGE_TOTAL, PATCH_TOKENS, D), 1.0, 6.0, ((0, 8), (1, 32)), (1, 2, 32, 2.75))
    output_weight = bell_draw(keys[6], (D, CH), CH ** -0.5, 0.25)
    return dict(patch_queries=patch_queries, patch_keys=patch_keys, scan_input=scan_input, decay_rate=decay_rate, gate_logit=gate_logit, grad_output=grad_output, output_weight=output_weight)


def compose(earlier, later):
    return (later[0] * earlier[0], later[0] * earlier[1] + later[1])


def silu_slope(gate_float):
    sigmoid_value = jax.nn.sigmoid(gate_float)
    return sigmoid_value * (1.0 + gate_float * (1.0 - sigmoid_value))


def head_backward(operands):
    query_head, key_head, value_head, grad_head = operands
    scaling = HEAD_DIM ** -0.5
    scores = jnp.dot(query_head, key_head.T, preferred_element_type=jnp.float32) * scaling
    log_total = jax.nn.logsumexp(scores, axis=1)
    weights = jnp.exp(scores - log_total[:, None])
    weights_low = weights.astype(jnp.bfloat16)
    attended = jnp.dot(weights_low, value_head, preferred_element_type=jnp.float32).astype(jnp.bfloat16)
    grad_weights = jnp.dot(grad_head, value_head.T, preferred_element_type=jnp.float32)
    row_delta = jnp.sum(weights * grad_weights, axis=1)
    weighted = (weights * grad_weights).astype(jnp.bfloat16)
    first_sum = jnp.dot(weighted, key_head, preferred_element_type=jnp.float32)
    second_sum = jnp.dot(weights_low, key_head, preferred_element_type=jnp.float32)
    grad_query = ((first_sum - row_delta[:, None] * second_sum) * scaling).astype(jnp.bfloat16)
    grad_scores = (weights * (grad_weights - row_delta[:, None])).astype(jnp.bfloat16)
    grad_key = (jnp.dot(grad_scores.T, query_head, preferred_element_type=jnp.float32) * scaling).astype(jnp.bfloat16)
    grad_value = jnp.dot(weights_low.T, grad_head, preferred_element_type=jnp.float32)
    return attended, grad_query, grad_key, grad_value


def split_heads(array):
    return array.reshape(array.shape[0], HEADS, HEAD_DIM).transpose(1, 0, 2)


def join_heads(array):
    return array.transpose(1, 0, 2).reshape(array.shape[1], HEADS * HEAD_DIM)


def image_backward(operands):
    query_image, key_image, value_image, grad_image = operands
    results = lax.map(head_backward, (split_heads(query_image), split_heads(key_image), split_heads(value_image), split_heads(grad_image)))
    return tuple(join_heads(result) for result in results)


def reference(patch_queries, patch_keys, scan_input, decay_rate, gate_logit, grad_output, output_weight):
    _, states = lax.associative_scan(compose, (decay_rate, scan_input), axis=1)
    gate_float = gate_logit.astype(jnp.float32)
    activation = jax.nn.silu(gate_float)
    value_low = (states * activation).astype(jnp.bfloat16)
    grad_attended = jnp.einsum("btd,dc->btc", grad_output.astype(jnp.float32), output_weight.astype(jnp.float32)).astype(jnp.bfloat16)
    attended, grad_queries, grad_keys, value_gradient = lax.map(image_backward, (patch_queries, patch_keys, value_low, grad_attended))
    grad_gate = (value_gradient * states * silu_slope(gate_float)).astype(jnp.bfloat16)
    shifted = jnp.concatenate([decay_rate[:, 1:], jnp.ones_like(decay_rate[:, :1])], axis=1)
    _, grad_input = lax.associative_scan(compose, (shifted, value_gradient * activation), reverse=True, axis=1)
    earlier = jnp.concatenate([jnp.zeros_like(states[:, :1]), states[:, :-1]], axis=1)
    grad_decay = grad_input * earlier
    grad_weight = jnp.einsum("btd,btc->dc", grad_output.astype(jnp.float32), attended.astype(jnp.float32))
    return grad_queries, grad_keys, grad_input, grad_decay, grad_gate, grad_weight
```

```python
import jax
import jax.numpy as jnp
from jax import lax
from jax.experimental import pallas as pl
from jax.experimental.pallas import tpu as pltpu
from jax.sharding import Mesh, PartitionSpec as P

HEADS = 8
HEAD_DIM = 64
ROWS = 128
CH = 512
PAIRS = CH // 128
ROW_AXES = ("y", "z", "core")
QBLOCK = 256
CHUNK = 256
SCALE = HEAD_DIM**-0.5


f32, bf16 = jnp.float32, jnp.bfloat16
NT = (((1,), (1,)), ((), ()))
TN = (((0,), (0,)), ((), ()))


def vmem(n):
    return [pl.BlockSpec(memory_space=pltpu.VMEM)] * n


def lanes_below(shape):
    return lax.broadcasted_iota(jnp.int32, shape, 1) < HEAD_DIM


def swap_halves(x):
    return pltpu.roll(x, HEAD_DIM, 1)


def sigmoid(z):
    return 1.0 / (1.0 + jnp.exp(-z))


def front_kernel(x_ref, decay_ref, go_ref, w_ref, state_ref, gain_ref, total_ref, grad_ref):
    row = lax.broadcasted_iota(jnp.int32, (ROWS, 128), 0)
    for p in range(PAIRS):
        part = pl.ds(128 * p, 128)
        x, g = x_ref[:, part], decay_ref[:, part]
        step = 1
        while step < ROWS:
            seen = row >= step
            x = x + g * jnp.where(seen, pltpu.roll(x, step, 0), 0.0)
            g = g * jnp.where(seen, pltpu.roll(g, step, 0), 1.0)
            step *= 2
        state_ref[:, part] = x
        gain_ref[:, part] = g
        total_ref[p : p + 1, :] = g[ROWS - 1 :, :]
        total_ref[PAIRS + p : PAIRS + p + 1, :] = x[ROWS - 1 :, :]
    grad_ref[...] = jnp.dot(go_ref[...], w_ref[...], preferred_element_type=f32).astype(bf16)


def value_kernel(
    index_ref, totals_ref, state_ref, gain_ref, gate_ref, q_ref, k_ref, g_ref,
    states_ref, incoming_ref, pack_ref,
):
    index = index_ref[0]

    def hop(at, carry):
        total = totals_ref[at]
        return jnp.where(at < index, total[:PAIRS] * carry + total[PAIRS:], carry)

    incoming = lax.fori_loop(0, totals_ref.shape[0], hop, jnp.zeros((PAIRS, 128), f32))
    below = lanes_below((ROWS, 128))
    for p in range(PAIRS):
        part = pl.ds(128 * p, 128)
        arriving = incoming[p : p + 1, :]
        incoming_ref[:, part] = jnp.broadcast_to(arriving, (8, 128))
        states = state_ref[:, part] + gain_ref[:, part] * arriving
        states_ref[:, part] = states
        z = gate_ref[:, part].astype(f32)
        value = states * (z * sigmoid(z))
        key, query = k_ref[:, part].astype(f32), q_ref[:, part].astype(f32)
        grad = g_ref[:, part].astype(f32)
        for piece, first, second in ((0, key, value), (1, query, grad)):
            pack_ref[2 * p, piece] = jnp.where(below, first, swap_halves(second)).astype(bf16)
            pack_ref[2 * p + 1, piece] = jnp.where(below, swap_halves(first), second).astype(bf16)


def attention_kernel(
    qg_ref, kv0_ref, kv1_ref, kv2_ref, kv3_ref,
    row_ref, out0_ref, out1_ref, out2_ref, out3_ref,
    kv, score, grad, key_sum, value_sum, attended, grad_query,
):
    step = pl.program_id(0)
    part = kv0_ref.shape[0]
    count = kv.shape[0] // CHUNK

    @pl.when(step == 0)
    def _():
        for number, ref in enumerate((kv0_ref, kv1_ref, kv2_ref, kv3_ref)):
            kv[pl.ds(number * part, part), :] = ref[...]
        key_sum[...] = jnp.zeros_like(key_sum)
        value_sum[...] = jnp.zeros_like(value_sum)

    qg = qg_ref[...].reshape(QBLOCK, 128)
    below = lanes_below((QBLOCK, 128))
    wide = qg.astype(f32)
    query = jnp.where(below, wide * SCALE, 0.0).astype(bf16)
    cotangent = jnp.where(below, 0.0, wide).astype(bf16)

    def rows_of(c):
        return pl.ds(pl.multiple_of(c * CHUNK, CHUNK), CHUNK)

    def fold(x, op):
        return op(x.reshape(CHUNK // 8, 8, QBLOCK), axis=0)

    def scores(c, top):
        s = lax.dot_general(kv[rows_of(c), :], query, NT, preferred_element_type=f32)
        score[rows_of(c), :] = s
        return jnp.maximum(top, fold(s, jnp.max))

    top = lax.fori_loop(0, count, scores, jnp.full((8, QBLOCK), -jnp.inf, f32))
    top = jnp.max(top, axis=0, keepdims=True)

    def exponents(c, total):
        e = jnp.exp(score[rows_of(c), :] - top)
        score[rows_of(c), :] = e
        return total + fold(e, jnp.sum)

    total = lax.fori_loop(0, count, exponents, jnp.zeros((8, QBLOCK), f32))
    inverse = 1.0 / jnp.sum(total, axis=0, keepdims=True)
    attended[...] = jnp.zeros_like(attended)
    grad_query[...] = jnp.zeros_like(grad_query)

    def forward(c, delta):
        rows = rows_of(c)
        block = kv[rows, :]
        weights = score[rows, :] * inverse
        low = weights.astype(bf16)
        gw = lax.dot_general(block, cotangent, NT, preferred_element_type=f32)
        score[rows, :] = weights
        grad[rows, :] = gw
        attended[...] += lax.dot_general(low, block, TN, preferred_element_type=f32)
        value_sum[rows, :] += jnp.dot(low, qg, preferred_element_type=f32)
        return delta + fold(weights * gw, jnp.sum)

    delta = lax.fori_loop(0, count, forward, jnp.zeros((8, QBLOCK), f32))
    delta = jnp.sum(delta, axis=0, keepdims=True)

    def backward(c, carry):
        rows = rows_of(c)
        low = (score[rows, :] * (grad[rows, :] - delta)).astype(bf16)
        grad_query[...] += lax.dot_general(low, kv[rows, :], TN, preferred_element_type=f32)
        key_sum[rows, :] += jnp.dot(low, qg, preferred_element_type=f32)
        return carry

    lax.fori_loop(0, count, backward, 0)
    row_ref[...] = jnp.where(below, grad_query[...] * SCALE, attended[...]).astype(bf16)

    @pl.when(step == pl.num_programs(0) - 1)
    def _():
        below = lanes_below((part, 128))
        for number, ref in enumerate((out0_ref, out1_ref, out2_ref, out3_ref)):
            rows = pl.ds(number * part, part)
            ref[...] = jnp.where(below, key_sum[rows, :] * SCALE, value_sum[rows, :])


def pair_of(ref, p, piece):
    first, second = ref[2 * p, piece].astype(f32), ref[2 * p + 1, piece].astype(f32)
    below = lanes_below((ROWS, 128))
    return (
        jnp.where(below, first, swap_halves(second)),
        jnp.where(below, swap_halves(first), second),
    )


def back_kernel(
    got_ref, decay_ref, gate_ref, states_ref,
    query_ref, key_ref, gate_grad_ref, adjoint_ref, tail_ref, total_ref, weight_ref,
):
    row = lax.broadcasted_iota(jnp.int32, (ROWS, 128), 0)
    for p in range(PAIRS):
        part = pl.ds(128 * p, 128)
        query, weight = pair_of(got_ref, p, 0)
        key, value = pair_of(got_ref, p, 1)
        query_ref[:, part] = query.astype(bf16)
        key_ref[:, part] = key.astype(bf16)
        weight_ref[:, part] = weight[: weight_ref.shape[0], :]
        z = gate_ref[:, part].astype(f32)
        s = sigmoid(z)
        slope = s * (1.0 + z * (1.0 - s))
        gate_grad_ref[:, part] = (value * states_ref[:, part] * slope).astype(bf16)
        decay = decay_ref[:, part]
        g = jnp.where(row < ROWS - 1, pltpu.roll(decay, ROWS - 1, 0), 1.0)
        x = value * (z * s)
        step = 1
        while step < ROWS:
            seen = row < ROWS - step
            x = x + g * jnp.where(seen, pltpu.roll(x, ROWS - step, 0), 0.0)
            g = g * jnp.where(seen, pltpu.roll(g, ROWS - step, 0), 1.0)
            step *= 2
        adjoint_ref[:, part] = x
        tail_ref[:, part] = g
        total_ref[p : p + 1, :] = decay[:1, :] * g[:1, :]
        total_ref[PAIRS + p : PAIRS + p + 1, :] = decay[:1, :] * x[:1, :]


def finish_kernel(
    index_ref, totals_ref, adjoint_ref, tail_ref, states_ref, incoming_ref, input_ref, decay_ref
):
    index = index_ref[0]
    length = totals_ref.shape[0]

    def hop(k, carry):
        at = length - 1 - k
        total = totals_ref[at]
        return jnp.where(at > index, total[:PAIRS] * carry + total[PAIRS:], carry)

    arriving = lax.fori_loop(0, length, hop, jnp.zeros((PAIRS, 128), f32))
    row = lax.broadcasted_iota(jnp.int32, (ROWS, 128), 0)
    for p in range(PAIRS):
        part = pl.ds(128 * p, 128)
        grad = adjoint_ref[:, part] + tail_ref[:, part] * arriving[p : p + 1, :]
        input_ref[:, part] = grad
        earlier = jnp.where(
            row > 0, pltpu.roll(states_ref[:, part], 1, 0), incoming_ref[0:1, part]
        )
        decay_ref[:, part] = grad * earlier


def shape(dims, dtype):
    return jax.ShapeDtypeStruct(dims, dtype)


def swap_core(x):
    return lax.ppermute(x, "core", [(0, 1), (1, 0)])


def swap_y(x):
    return lax.ppermute(x, "y", [(0, 1), (1, 0)])


def everyone(total, count):
    return lax.all_to_all(jnp.broadcast_to(total[None], (count,) + total.shape), ROW_AXES, 0, 0)


def body(queries, keys, scan_input, decay_rate, gate_logit, grad_output, output_weight):
    queries, keys, scan_input, decay, gate, grad_output = (
        array[0]
        for array in (queries, keys, scan_input, decay_rate, gate_logit, grad_output)
    )
    ny, nz, nc = (lax.axis_size(name) for name in ROW_AXES)
    ndp = lax.axis_size("dp")
    count = ny * nz * nc
    width = grad_output.shape[1]
    index = lax.axis_index(ROW_AXES).reshape(1)
    flat = shape((ROWS, CH), f32)
    low = shape((ROWS, CH), bf16)
    scalar = [pl.BlockSpec(memory_space=pltpu.SMEM)]

    local, gain, total, grad_attended = pl.pallas_call(
        front_kernel,
        name="front",
        out_shape=(flat, flat, shape((2 * PAIRS, 128), f32), low),
        in_specs=vmem(4),
        out_specs=tuple(vmem(4)),
    )(scan_input, decay, grad_output, output_weight)
    totals = everyone(total, count)
    states, incoming, pack = pl.pallas_call(
        value_kernel,
        name="value",
        out_shape=(flat, shape((8, CH), f32), shape((HEADS, 2, ROWS, 128), bf16)),
        in_specs=scalar + vmem(7),
        out_specs=tuple(vmem(3)),
    )(index, totals, local, gain, gate, queries, keys, grad_attended)

    gathered_output = lax.all_gather(grad_output, "z", axis=0, tiled=True)

    got = lax.all_to_all(pack, "z", 0, 0)
    own = got[:, 0].reshape(nz * ROWS, 128)
    across = swap_y(own)
    beside = swap_core(own)
    diagonal = swap_core(across)
    part = nz * ROWS
    whole = pl.BlockSpec((part, 128), lambda i: (0, 0))
    rows, own_sum, beside_sum, across_sum, diagonal_sum = pl.pallas_call(
        attention_kernel,
        name="attention",
        grid=(part // QBLOCK,),
        out_shape=(shape((part, 128), bf16),) + (shape((part, 128), f32),) * 4,
        in_specs=[
            pl.BlockSpec((QBLOCK // ROWS, None, ROWS, 128), lambda i: (i, 1, 0, 0)),
            whole, whole, whole, whole,
        ],
        out_specs=(pl.BlockSpec((QBLOCK, 128), lambda i: (i, 0)), whole, whole, whole, whole),
        scratch_shapes=[
            pltpu.VMEM((4 * part, 128), bf16),
            pltpu.VMEM((4 * part, QBLOCK), f32),
            pltpu.VMEM((4 * part, QBLOCK), f32),
            pltpu.VMEM((4 * part, 128), f32),
            pltpu.VMEM((4 * part, 128), f32),
            pltpu.VMEM((QBLOCK, 128), f32),
            pltpu.VMEM((QBLOCK, 128), f32),
        ],
    )(got, own, beside, across, diagonal)

    weight = lax.dot_general(
        gathered_output, rows, TN, preferred_element_type=f32
    ).reshape(ndp, ny, nz, nc, width // (ndp * count), 128)
    y, core = lax.axis_index("y"), lax.axis_index("core")

    def pick(x, at, axis):
        return lax.dynamic_index_in_dim(x, at, axis, keepdims=False)

    own_sum = own_sum + swap_core(beside_sum)
    across_sum = across_sum + swap_core(diagonal_sum)
    own_sum = own_sum + swap_y(across_sum)
    weight = pick(weight, core, 3) + swap_core(pick(weight, 1 - core, 3))
    weight = pick(weight, y, 1) + swap_y(pick(weight, 1 - y, 1))
    piece = weight.transpose(1, 0, 2, 3).reshape(nz, -1, 128)
    piece = jnp.pad(piece, ((0, 0), (0, ROWS - piece.shape[1]), (0, 0)))
    below = jnp.arange(128) < HEAD_DIM
    first = jnp.where(below, rows.reshape(nz, ROWS, 128), piece.astype(bf16))
    second = own_sum.astype(bf16).reshape(nz, ROWS, 128)
    got = lax.all_to_all(jnp.stack([first, second], axis=1), "z", 0, 0)

    held = width // count
    grad_queries, grad_keys, grad_gate, adjoint, tail, total, weight = pl.pallas_call(
        back_kernel,
        name="back",
        out_shape=(low, low, low, flat, flat, shape((2 * PAIRS, 128), f32), shape((held, CH), f32)),
        in_specs=vmem(4),
        out_specs=tuple(vmem(7)),
    )(got, decay, gate, states)
    totals = everyone(total, count)
    grad_input, grad_decay = pl.pallas_call(
        finish_kernel,
        name="finish",
        out_shape=(flat, flat),
        in_specs=scalar + vmem(5),
        out_specs=tuple(vmem(2)),
    )(index, totals, adjoint, tail, states, incoming)
    grad_weight = jnp.sum(
        lax.all_to_all(weight.reshape(ndp, held // ndp, CH), "dp", 0, 0), axis=0
    )
    return (
        grad_queries[None], grad_keys[None], grad_input[None], grad_decay[None],
        grad_gate[None], grad_weight,
    )


def solution(mesh):
    devices = mesh.devices
    row = devices.shape[1]
    fine = Mesh(devices.reshape(devices.shape[0], 2, row // 4, 2), ("dp",) + ROW_AXES)
    rows = P("dp", ROW_AXES, None)
    return jax.shard_map(
        body,
        mesh=fine,
        in_specs=(rows,) * 6 + (P(),),
        out_specs=(rows,) * 5 + (P(("dp",) + ROW_AXES, None),),
        check_vma=False,
    )
```
